32 devices in a mesh: gx: 4 (over y, x), gy: 2 (over core), gz: 4 (over z).
Axes of the slice: x: 2, y: 2, z: 4, core: 2. Of those that a mesh axis runs over, the one named last changes fastest.
Arguments:
- thermal_field: float32 [32, 32, 512], P('gz', 'gy', 'gx'), may hold values from -2 to 4
- forcing_per_step: float32 [32, 32, 512], P('gz', 'gy', 'gx'), may hold values from 0.1 to 4
- substance_label: int32 [32, 32, 512], P('gz', 'gy', 'gx'), may hold values from 0 to 7
- thermal_conductivities: float32 [8], replicated, may hold values from 0.5 to 4
- patch_group_label: int32 [4, 4, 16], P('gz', 'gy', 'gx'), may hold values from 0 to 63, as said below
- drain_power_density: float32 [64], replicated, may hold values from 0.2 to 2
Outputs:
- next_thermal_field: float32 [32, 32, 512], P('gz', 'gy', 'gx')
- forcing_with_drain: float32 [32, 32, 512], P('gz', 'gy', 'gx')
The draws below stay inside these ranges and needn't reach their ends.
Inputs may be any that keep to these rules, and one draw needn't show every extreme that they name: `patch_group_label`: every cluster labels exactly four tiles.
All inputs are finite; a program needn't handle non-finite values.
Results may differ from the reference program's by a relative error of at most 0.0003.
Values sent between devices are 32-bit elements; how exact they have to be, the bound alone decides.
A program may use at most 64 MiB of HBM per device.

```python
import math
import jax
import jax.numpy as jnp
from jax import lax

CZ = 8
TX = 32
TY = 8
NMAT = 8
NX = 512
NY = 32
NZ = 32
CLUSTERS = 64


def draw_thermal_field(key, part):
    base_key = jax.random.fold_in(key, 11)
    noise_key = jax.random.fold_in(key, 12)
    tiles = (NZ // CZ, NY // TY, NX // TX)
    base = jax.random.uniform(base_key, tiles, jnp.float32, 0.0, 2.0)
    noise = jnp.clip(0.5 * jax.random.normal(noise_key, (NZ, NY, NX), jnp.float32), -1.5, 1.5)
    spread = jnp.repeat(jnp.repeat(jnp.repeat(base, CZ, 0), TY, 1), TX, 2)
    return spread + noise


def draw_patch_group_label(key, part):
    count = NZ // CZ * (NY // TY) * (NX // TX)
    order = jax.random.permutation(jax.random.fold_in(key, 21), count)
    return (order // 4).astype(jnp.int32).reshape(NZ // CZ, NY // TY, NX // TX)


def plant(array, rng, smallest, largest):
    longest = array.shape.index(max(array.shape))
    spots = []
    for shift in (0, 1):
        where = [jax.random.randint(jax.random.fold_in(rng, axis), (), 0, length) for axis, length in enumerate(array.shape)]
        where[longest] = (where[longest] + shift) % array.shape[longest]
        spots.append(tuple(where))
    return array.at[spots[0]].set(smallest).at[spots[1]].set(largest)


def steps_of(key, extent, cuts, least, high):
    factor_of, own = 1.0, jax.random.fold_in(key, 6)
    for dim, parts in cuts:
        steps = jnp.exp(jax.random.uniform(jax.random.fold_in(own, dim), (parts,), jnp.float32, least / len(cuts), high / len(cuts)))
        factor_of = factor_of * jnp.repeat(steps, extent[dim] // parts).reshape([-1 if axis == dim else 1 for axis in range(len(extent))])
    return factor_of


def setup_inputs(seed: int = 0) -> dict:
    arg_keys = jax.random.split(jax.random.key(seed), 7)
    thermal_field = draw_thermal_field(jax.random.fold_in(arg_keys[6], 71), 0)
    forcing_per_step = jnp.clip(jnp.exp(math.log(4.0) - 3.6888794 * jax.random.uniform(arg_keys[1], (NZ, NY, NX), jnp.float32) ** steps_of(arg_keys[1], (NZ, NY, NX), ((0, 4), (1, 2), (2, 4)), -0.2, 0.2)), 0.1, 4.0)
    substance_label = plant(jax.random.randint(arg_keys[2], (NZ, NY, NX), 0, NMAT), jax.random.fold_in(arg_keys[2], 1), 0, NMAT - 1).astype(jnp.int32)
    thermal_conductivities = jnp.clip(jnp.exp(jax.random.uniform(arg_keys[3], (NMAT,), jnp.float32, math.log(0.5), math.log(4.0))), 0.5, 4.0)
    patch_group_label = draw_patch_group_label(jax.random.fold_in(arg_keys[6], 71), 0)
    drain_power_density = jnp.clip(jnp.exp(jax.random.uniform(arg_keys[5], (CLUSTERS,), jnp.float32, math.log(0.2), math.log(2.0))), 0.2, 2.0)
    return dict(thermal_field=thermal_field, forcing_per_step=forcing_per_step, substance_label=substance_label, thermal_conductivities=thermal_conductivities, patch_group_label=patch_group_label, drain_power_density=drain_power_density)


IMPLICIT_WEIGHT = 0.5
LATERAL_RATE = 100.0
VERTICAL_RATE = 400.0
SOURCE_STEP = 0.5
LEAK_SLOPE = 0.5

def harmonic(first_k, second_k):
    return 2.0 * first_k * second_k / (first_k + second_k)

def line_sweep(right_side, face, axis_pos):
    moved = jnp.moveaxis(right_side, axis_pos, -1)
    moved_face = jnp.moveaxis(face, axis_pos, -1)
    lower_band = -IMPLICIT_WEIGHT * moved_face[..., :-1]
    upper_band = -IMPLICIT_WEIGHT * moved_face[..., 1:]
    main_band = 1.0 + IMPLICIT_WEIGHT * (moved_face[..., :-1] + moved_face[..., 1:])
    solved = lax.linalg.tridiagonal_solve(lower_band, main_band, upper_band, moved[..., None])[..., 0]
    return jnp.moveaxis(solved, -1, axis_pos)

def reference(thermal_field, forcing_per_step, substance_label, thermal_conductivities, patch_group_label, drain_power_density):
    voxel_thermal_link = jnp.zeros(thermal_field.shape, jnp.float32)
    for level in range(NMAT):
        voxel_thermal_link = voxel_thermal_link + jnp.where(substance_label == level, thermal_conductivities[level], 0.0)
    padk = jnp.pad(voxel_thermal_link, 1)
    sideways_link_xaxis = LATERAL_RATE * harmonic(padk[1:-1, 1:-1, :-1], padk[1:-1, 1:-1, 1:])
    sideways_link_yaxis = LATERAL_RATE * harmonic(padk[1:-1, :-1, 1:-1], padk[1:-1, 1:, 1:-1])
    upward_link_strength = VERTICAL_RATE * harmonic(padk[:-1, 1:-1, 1:-1], padk[1:, 1:-1, 1:-1])
    bordered_thermal_field = jnp.pad(thermal_field, 1)
    diagonal_coefficient = thermal_field
    energy_current = sideways_link_xaxis[:, :, 1:] * (bordered_thermal_field[1:-1, 1:-1, 2:] - diagonal_coefficient) - sideways_link_xaxis[:, :, :-1] * (diagonal_coefficient - bordered_thermal_field[1:-1, 1:-1, :-2])
    energy_current = energy_current + sideways_link_yaxis[:, 1:, :] * (bordered_thermal_field[1:-1, 2:, 1:-1] - diagonal_coefficient) - sideways_link_yaxis[:, :-1, :] * (diagonal_coefficient - bordered_thermal_field[1:-1, :-2, 1:-1])
    energy_current = energy_current + upward_link_strength[1:] * (bordered_thermal_field[2:, 1:-1, 1:-1] - diagonal_coefficient) - upward_link_strength[:-1] * (diagonal_coefficient - bordered_thermal_field[:-2, 1:-1, 1:-1])
    residual = SOURCE_STEP * forcing_per_step + energy_current
    step_x = line_sweep(residual, sideways_link_xaxis, 2)
    step_y = line_sweep(step_x, sideways_link_yaxis, 1)
    upward_correction = line_sweep(step_y, upward_link_strength, 0)
    next_thermal_field = thermal_field + upward_correction
    patch_extents = (NZ // CZ, CZ, NY // TY, TY, NX // TX, TX)
    patch_power_sum = next_thermal_field.reshape(patch_extents).sum(axis=(1, 3, 5))
    cluster_total = jax.ops.segment_sum(patch_power_sum.reshape(-1), patch_group_label.reshape(-1), CLUSTERS)
    cluster_mean = cluster_total / (4 * CZ * TY * TX)
    leak_power = drain_power_density * jnp.exp(LEAK_SLOPE * cluster_mean)
    tile_power = leak_power[patch_group_label]
    forcing_with_drain = forcing_per_step.reshape(patch_extents) + tile_power[:, None, :, None, :, None]
    return (next_thermal_field, forcing_with_drain.reshape(forcing_per_step.shape))
```

```python
import functools

import jax
import jax.numpy as jnp
from jax import lax
from jax.experimental import pallas as pl
from jax.experimental.pallas import tpu as pltpu
from jax.sharding import PartitionSpec as P

TX = 32
TY = 8
LATERAL_RATE = 100.0
VERTICAL_RATE = 400.0
LEAK_SLOPE = 0.5
AXES = ("gx", "gy", "gz")
MESH = pl.DeviceIdType.MESH


def down(v, s):
    n = v.shape[0]
    s = s % n
    if s == 0:
        return v
    if v.ndim == 2 and s % 8:
        return pltpu.roll(v, s, 0)
    return jnp.concatenate([v[n - s:], v[: n - s]], axis=0)


def up(v, s):
    return down(v, v.shape[0] - s % v.shape[0])


def half_face(k, rate):
    below = down(k, 1)
    face = rate * k * below / (k + below)
    return jnp.where(lax.broadcasted_iota(jnp.int32, k.shape, 0) == 0, 0.0, face)


def factor(a):
    n = a.shape[0]
    rows = lax.broadcasted_iota(jnp.int32, a.shape, 0)
    first = jnp.where(rows == 0, 1.0, 0.0)
    last = jnp.where(rows == n - 1, 1.0, 0.0)
    excess = jnp.ones_like(a)
    b = up(a, 1)
    stages = []
    s = 1
    while s < n:
        inv = 1.0 / (excess + a + b)
        fd = a * down(inv, s)
        fu = b * up(inv, s)
        stages.append((s, fd, fu))
        excess = excess + fd * down(excess, s) + fu * up(excess, s)
        first = first + fd * down(first, s) + fu * up(first, s)
        last = last + fd * down(last, s) + fu * up(last, s)
        a = fd * down(a, s)
        b = up(a, 2 * s)
        s *= 2
    inv = 1.0 / excess
    return stages, inv, first * inv, last * inv


def apply_stages(stages, inv, r):
    for s, fd, fu in stages:
        r = r + fd * down(r, s) + fu * up(r, s)
    return r * inv


def chain_factor(mats):
    out = []
    slope = None
    for i in range(len(mats) - 1):
        den = mats[i][0] + mats[i + 1][1]
        if slope is not None:
            den = den - mats[i][2] * slope
        inv = 1.0 / den
        slope = mats[i + 1][2] * inv
        out.append((inv, slope, mats[i][2]))
    return out


def chain_flux(elim, firsts, lasts):
    ys = []
    for i, (inv, _, cross) in enumerate(elim):
        rhs = lasts[i] - firsts[i + 1]
        if i:
            rhs = rhs + cross * ys[-1]
        ys.append(rhs * inv)
    qs = [None] * len(ys)
    for i in reversed(range(len(ys))):
        qs[i] = ys[i] if i == len(ys) - 1 else ys[i] + elim[i][1] * qs[i + 1]
    return qs


def pick(values, index):
    out = jnp.zeros_like(values[0])
    for i, value in enumerate(values):
        out = jnp.where(index == i, value, out)
    return out


def kernel(sizes, clusters, cond_ref, label_ref, dens_ref, t_hbm, f_hbm, m_hbm, next_hbm, force_hbm,
           t_v, f_v, m_v, k_v, flux_v, hxs, hxr, hys, hyr, hzs, hzr, xm, ym, zm, xb, yb, zb, lab, cbuf,
           out_v, fout_v, in_sem, out_sem, hs_sem, hr_sem, *sems):
    nx, ny, nz = sizes
    me = {axis: lax.axis_index(axis) for axis in AXES}
    count = dict(zip(AXES, sizes))
    cz, cy, cx = 8, 16, 128
    lines = cz * cy

    def target(axes, index):
        ids = dict(me)
        for axis in reversed(axes):
            ids[axis] = lax.rem(index, count[axis])
            index = index // count[axis]
        return tuple(ids[axis] for axis in AXES)

    def place(axes):
        n, here = 1, 0
        for axis in axes:
            n, here = n * count[axis], here * count[axis] + me[axis]
        return n, here

    stages_c = [("gx", "gy")] if nx * ny <= 16 else [("gx",), ("gy",)]
    hxr[...] = jnp.zeros_like(hxr)
    hyr[...] = jnp.zeros_like(hyr)
    hzr[...] = jnp.zeros_like(hzr)
    barrier = pltpu.get_barrier_semaphore()
    greeted = 0
    plane = ("gx", "gy") if nx * ny <= 16 else None
    groups = [plane, ("gz",)] if plane else [("gx",), ("gy",), ("gz",)]
    for axes in groups:
        n, here = place(axes)
        for d in range(1, n):
            pl.semaphore_signal(barrier, inc=1, device_id=target(axes, lax.rem(here + d, n)),
                                device_id_type=MESH)
            greeted += 1
    ins = [pltpu.make_async_copy(s, d, in_sem.at[i])
           for i, (s, d) in enumerate(((m_hbm, m_v), (t_hbm, t_v), (f_hbm, f_v)))]
    for c in ins:
        c.start()

    finish = []

    class Gather:
        def __init__(self, buf, axes, ssem, rsem):
            self.buf, self.axes, self.ssem, self.rsem = buf, axes, ssem, rsem
            self.n, self.here = place(axes)

        def copy(self, d, slot):
            return pltpu.make_async_remote_copy(
                src_ref=self.buf.at[slot], dst_ref=self.buf.at[slot], send_sem=self.ssem.at[d - 1],
                recv_sem=self.rsem.at[slot], device_id=target(self.axes, lax.rem(self.here + d, self.n)),
                device_id_type=MESH)

        def start(self):
            for d in range(1, self.n):
                c = self.copy(d, self.here)
                c.start()
                finish.append(c)

        def wait(self):
            for d in range(1, self.n):
                self.copy(d, lax.rem(self.here + self.n - d, self.n)).wait_recv()

    gathers = []
    specs = [(xm, ("gx",)), (ym, ("gy",)), (zm, ("gz",)), (xb, ("gx",)), (yb, ("gy",)), (zb, ("gz",)),
             (lab, ("gz",))]
    for i, (buf, axes) in enumerate(specs):
        gathers.append(Gather(buf, axes, sems[2 * i], sems[2 * i + 1]))
    gxm, gym, gzm, gxb, gyb, gzb, glab = gathers

    rows8 = lax.broadcasted_iota(jnp.int32, (8, 128), 0)
    lanes8 = lax.broadcasted_iota(jnp.int32, (8, 128), 1)
    own_label = jnp.zeros((8, 128), jnp.float32)
    for t in range(8):
        own_label = jnp.where(rows8 == t, label_ref[0, t // 4, t % 4].astype(jnp.float32), own_label)
    lab[me["gz"]] = own_label

    ins[0].wait()
    material = m_v[...]
    k = jnp.zeros(material.shape, jnp.float32)
    for level in range(8):
        k = jnp.where(material == level, cond_ref[level], k)
    k_v[...] = k
    ins[1].wait()

    def yz(ref):
        return jnp.concatenate([ref[pl.ds(y, cz, stride=cy), :][None] for y in range(cy)], axis=0)

    k_yz, t_yz = yz(k_v), yz(t_v)
    k_x = k_yz.reshape(lines, cx).T
    t_x = t_yz.reshape(lines, cx).T
    k_zy, t_zy = k.reshape(cz, cy, cx), t_v[...].reshape(cz, cy, cx)
    for axis_k, axis_t, buf in ((k_x, t_x, hxs), (k_yz, t_yz, hys), (k_zy, t_zy, hzs)):
        n = axis_k.shape[0]
        for side, at in ((0, 0), (1, n - 1)):
            if axis_k.ndim == 2:
                buf[side, 0:1] = axis_k[at:at + 1]
                buf[side, 1:2] = axis_t[at:at + 1]
            else:
                buf[side, 0] = axis_k[at]
                buf[side, 1] = axis_t[at]

    pl.semaphore_wait(barrier, greeted)

    halos = []
    for i, (axis, sbuf, rbuf) in enumerate((("gx", hxs, hxr), ("gy", hys, hyr), ("gz", hzs, hzr))):
        n, here = count[axis], me[axis]
        for side in (0, 1):
            other = lax.rem(here + (1 if side else n - 1), n)
            c = pltpu.make_async_remote_copy(
                src_ref=sbuf.at[side], dst_ref=rbuf.at[1 - side], send_sem=hs_sem.at[2 * i + side],
                recv_sem=hr_sem.at[2 * i + 1 - side], device_id=target((axis,), other), device_id_type=MESH)
            r = pltpu.make_async_remote_copy(
                src_ref=sbuf.at[side], dst_ref=rbuf.at[side], send_sem=hs_sem.at[2 * i + side],
                recv_sem=hr_sem.at[2 * i + side], device_id=target((axis,), other), device_id_type=MESH)
            has = here < n - 1 if side else here > 0
            halos.append((has, c, r))
            pl.when(has)(c.start)
    glab.start()

    a_x = half_face(k_x, LATERAL_RATE)
    a_y = half_face(k_yz, LATERAL_RATE)
    a_z = half_face(k_zy, VERTICAL_RATE)

    def ends(first, last, kk, rate):
        n = first.shape[0]
        return (last[n - 1:] + 1.0 / (rate * kk[n - 1:]), first[:1] + 1.0 / (rate * kk[:1]), first[n - 1:])

    def put3(buf, here, parts):
        for i, part in enumerate(parts):
            if part.ndim == 2:
                buf[here, i:i + 1] = part
            else:
                buf[here, i] = part[0]

    def get(buf, i, j):
        return buf[i, j:j + 1] if len(buf.shape) == 3 else buf[i, j][None]

    stages_x, inv_x, first_x, last_x = factor(a_x)
    put3(xm, me["gx"], ends(first_x, last_x, k_x, LATERAL_RATE))
    gxm.start()

    def inner_flux(a, t):
        flow = 2.0 * a * (t - down(t, 1))
        return up(flow, 1) - flow

    ins[2].wait()
    flux_x = inner_flux(a_x, t_x)
    flux_y = inner_flux(a_y, t_yz) + 0.5 * yz(f_v)
    flux_z = inner_flux(a_z, t_zy)

    for has, c, r in halos:
        pl.when(has)(r.wait_recv)

    def halo_flux(k_own, t_own, k_far, t_far, rate):
        return 2.0 * rate * k_own * k_far / (k_own + k_far) * (t_far - t_own)

    def with_halo(flux, kk, tt, buf, rate):
        n = flux.shape[0]
        get_h = lambda side, j: buf[side, j:j + 1] if flux.ndim == 2 else buf[side, j][None]
        low = halo_flux(kk[:1], tt[:1], get_h(0, 0), get_h(0, 1), rate)
        high = halo_flux(kk[n - 1:], tt[n - 1:], get_h(1, 0), get_h(1, 1), rate)
        if flux.ndim == 2:
            rows = lax.broadcasted_iota(jnp.int32, flux.shape, 0)
            return flux + jnp.where(rows == 0, low, 0.0) + jnp.where(rows == n - 1, high, 0.0)
        return jnp.concatenate([flux[:1] + low, flux[1:n - 1], flux[n - 1:] + high], axis=0)

    flux_v[...] = with_halo(flux_z, k_zy, t_zy, hzr, VERTICAL_RATE).reshape(lines, cx)
    flux_y = with_halo(flux_y, k_yz, t_yz, hyr, LATERAL_RATE) + yz(flux_v)
    residual = with_halo(flux_x, k_x, t_x, hxr, LATERAL_RATE) + flux_y.reshape(lines, cx).T

    r_x = apply_stages(stages_x, inv_x, residual)
    put3(xb, me["gx"], (r_x[:1], r_x[cx - 1:]))
    gxb.start()

    stages_y, inv_y, first_y, last_y = factor(a_y)
    put3(ym, me["gy"], ends(first_y, last_y, k_yz, LATERAL_RATE))
    gym.start()
    gxm.wait()
    elim_x = chain_factor([tuple(get(xm, i, j) for j in range(3)) for i in range(nx)])
    gxb.wait()

    def join(buf, n, elim, r, first, last, here):
        qs = chain_flux(elim, [get(buf, i, 0) for i in range(n)], [get(buf, i, 1) for i in range(n)])
        if not qs:
            return r, qs
        return r + pick(qs, here - 1) * first - pick(qs, here) * last, qs

    step, _ = join(xb, nx, elim_x, r_x, first_x, last_x, me["gx"])
    r_y = apply_stages(stages_y, inv_y, step.T.reshape(cy, cz, cx))
    put3(yb, me["gy"], (r_y[:1], r_y[cy - 1:]))
    gyb.start()

    stages_z, inv_z, first_z, last_z = factor(a_z)
    put3(zm, me["gz"], ends(first_z, last_z, k_zy, VERTICAL_RATE))
    gzm.start()
    gym.wait()
    elim_y = chain_factor([tuple(get(ym, i, j) for j in range(3)) for i in range(ny)])
    gyb.wait()
    step, _ = join(yb, ny, elim_y, r_y, first_y, last_y, me["gy"])
    for y in range(cy):
        flux_v[pl.ds(y, cz, stride=cy), :] = step[y]
    rhs_z = flux_v[...].reshape(cz, cy, cx)
    r_z = apply_stages(stages_z, inv_z, rhs_z)
    put3(zb, me["gz"], (r_z[:1], r_z[cz - 1:], jnp.sum(t_zy + rhs_z, axis=0, keepdims=True)))
    gzb.start()

    gzm.wait()
    elim_z = chain_factor([tuple(get(zm, i, j) for j in range(3)) for i in range(nz)])
    glab.wait()
    width = cbuf.shape[-1] if len(cbuf.shape) == 3 else 128
    ids = lax.broadcasted_iota(jnp.int32, (8, width), 1).astype(jnp.float32)

    def onehot(labels):
        return jnp.concatenate([labels] * (width // 128), axis=1) == ids

    in_tile = lanes8 // TX == rows8 % 4
    gzb.wait()
    step, qs = join(zb, nz, elim_z, r_z, first_z, last_z, me["gz"])

    total = jnp.zeros((8, width), jnp.float32)
    for i in range(nz):
        cells = get(zb, i, 2)[0]
        if i > 0:
            cells = cells + qs[i - 1][0]
        if i < nz - 1:
            cells = cells - qs[i][0]
        upper = jnp.sum(cells[:TY], axis=0, keepdims=True)
        lower = jnp.sum(cells[TY:], axis=0, keepdims=True)
        tiles = jnp.where(in_tile, jnp.where(rows8 < 4, upper, lower), 0.0)
        sums = jnp.sum(tiles, axis=1, keepdims=True)
        total = total + jnp.where(onehot(lab[i]), sums, 0.0)
    total = jnp.sum(total, axis=0, keepdims=True)
    base = 0
    for j, axes in enumerate(stages_c):
        n, here = place(axes)
        part = Gather(cbuf.at[pl.ds(base, n)], axes, sems[14 + 2 * j], sems[15 + 2 * j])
        cbuf[base + here, 0:1] = total
        part.start()
        if j == 0:
            out_v[...] = (t_zy + step).reshape(lines, cx)
            out0 = pltpu.make_async_copy(out_v, next_hbm, out_sem.at[0])
            out0.start()
        part.wait()
        total = cbuf[base, 0:1]
        for i in range(1, n):
            total = total + cbuf[base + i, 0:1]
        base += n

    mean = total / (4 * cz * TY * TX)
    leak = dens_ref[...] * jnp.exp(LEAK_SLOPE * mean[:, :clusters])
    power = jnp.sum(jnp.where(onehot(own_label)[:, :clusters], leak, 0.0), axis=1, keepdims=True)
    spread = jnp.where(in_tile, power, 0.0)
    upper = jnp.sum(spread[:4], axis=0, keepdims=True)
    lower = jnp.sum(spread[4:], axis=0, keepdims=True)
    rows16 = lax.broadcasted_iota(jnp.int32, (cy, cx), 0)
    layer = jnp.where(rows16 < TY, upper, lower)
    fout_v[...] = (f_v[...].reshape(cz, cy, cx) + layer[None]).reshape(lines, cx)
    out1 = pltpu.make_async_copy(fout_v, force_hbm, out_sem.at[1])
    out1.start()

    for has, c, r in halos:
        pl.when(has)(c.wait_send)
    for c in finish:
        c.wait_send()
    out0.wait()
    out1.wait()


def per_device(sizes, thermal_field, forcing_per_step, substance_label, thermal_conductivities,
               patch_group_label, drain_power_density):
    nx, ny, nz = sizes
    shape = thermal_field.shape
    cz, cy, cx = shape
    lines = cz * cy
    clusters = drain_power_density.shape[0]
    width = -(-clusters // 128) * 128
    f32 = jnp.float32
    flat = lambda v: v.reshape(lines, cx)
    vm = lambda *s: pltpu.VMEM(s, f32)
    dma = pltpu.SemaphoreType.DMA
    small = nx * ny <= 16
    csizes = [nx * ny] if small else [nx, ny]
    sems = []
    for n in [nx, ny, nz, nx, ny, nz, nz] + csizes:
        sems += [dma((max(n - 1, 1),)), dma((n,))]
    any_spec = pl.BlockSpec(memory_space=pl.ANY)
    smem = pl.BlockSpec(memory_space=pltpu.SMEM)
    new, force = pl.pallas_call(
        functools.partial(kernel, sizes, clusters),
        out_shape=[jax.ShapeDtypeStruct((lines, cx), f32)] * 2,
        in_specs=[smem, smem, pl.BlockSpec(memory_space=pltpu.VMEM), any_spec, any_spec, any_spec],
        out_specs=[any_spec, any_spec],
        scratch_shapes=[
            vm(lines, cx), vm(lines, cx), pltpu.VMEM((lines, cx), jnp.int32), vm(lines, cx), vm(lines, cx),
            vm(2, 2, lines), vm(2, 2, lines), vm(2, 2, cz, cx), vm(2, 2, cz, cx), vm(2, 2, cy, cx), vm(2, 2, cy, cx),
            vm(nx, 8, lines), vm(ny, 3, cz, cx), vm(nz, 3, cy, cx),
            vm(nx, 8, lines), vm(ny, 2, cz, cx), vm(nz, 3, cy, cx),
            vm(nz, 8, 128), vm(sum(csizes), 8, width),
            vm(lines, cx), vm(lines, cx),
            dma((3,)), dma((2,)), dma((6,)), dma((6,)),
        ] + sems,
        compiler_params=pltpu.CompilerParams(collective_id=0, has_side_effects=True),
    )(thermal_conductivities, patch_group_label, drain_power_density.reshape(1, clusters),
      flat(thermal_field), flat(forcing_per_step), flat(substance_label))
    return new.reshape(shape), force.reshape(shape)


def solution(mesh):
    block = P("gz", "gy", "gx")
    return jax.shard_map(
        functools.partial(per_device, tuple(mesh.shape[axis] for axis in AXES)),
        mesh=mesh, in_specs=(block, block, block, P(), block, P()), out_specs=(block, block), check_vma=False,
    )
```

```python
import functools

import jax
import jax.numpy as jnp
from jax import lax
from jax.experimental import pallas as pl
from jax.experimental.pallas import tpu as pltpu
from jax.sharding import PartitionSpec as P

TX = 32
TY = 8
LATERAL_RATE = 100.0
VERTICAL_RATE = 400.0
LEAK_SLOPE = 0.5
AXES = ("gx", "gy", "gz")
MESH = pl.DeviceIdType.MESH


def down(v, s):
    n = v.shape[0]
    s = s % n
    if s == 0:
        return v
    if v.ndim == 2 and s % 8:
        return pltpu.roll(v, s, 0)
    return jnp.concatenate([v[n - s:], v[: n - s]], axis=0)


def up(v, s):
    return down(v, v.shape[0] - s % v.shape[0])


def half_face(k, rate):
    below = down(k, 1)
    face = rate * k * below / (k + below)
    return jnp.where(lax.broadcasted_iota(jnp.int32, k.shape, 0) == 0, 0.0, face)


def factor(a):
    n = a.shape[0]
    rows = lax.broadcasted_iota(jnp.int32, a.shape, 0)
    first = jnp.where(rows == 0, 1.0, 0.0)
    last = jnp.where(rows == n - 1, 1.0, 0.0)
    excess = jnp.ones_like(a)
    b = up(a, 1)
    stages = []
    s = 1
    while s < n:
        inv = 1.0 / (excess + a + b)
        fd = a * down(inv, s)
        fu = b * up(inv, s)
        stages.append((s, fd, fu))
        excess = excess + fd * down(excess, s) + fu * up(excess, s)
        first = first + fd * down(first, s) + fu * up(first, s)
        last = last + fd * down(last, s) + fu * up(last, s)
        a = fd * down(a, s)
        b = up(a, 2 * s)
        s *= 2
    inv = 1.0 / excess
    return stages, inv, first * inv, last * inv


def apply_stages(stages, inv, r):
    for s, fd, fu in stages:
        r = r + fd * down(r, s) + fu * up(r, s)
    return r * inv


def chain_factor(mats):
    out = []
    slope = None
    for i in range(len(mats) - 1):
        den = mats[i][0] + mats[i + 1][1]
        if slope is not None:
            den = den - mats[i][2] * slope
        inv = 1.0 / den
        slope = mats[i + 1][2] * inv if i < len(mats) - 2 else None
        out.append((inv, slope, mats[i][2]))
    return out


def chain_flux(elim, firsts, lasts):
    ys = []
    for i, (inv, _, cross) in enumerate(elim):
        rhs = lasts[i] - firsts[i + 1]
        if i:
            rhs = rhs + cross * ys[-1]
        ys.append(rhs * inv)
    qs = [None] * len(ys)
    for i in reversed(range(len(ys))):
        qs[i] = ys[i] if i == len(ys) - 1 else ys[i] + elim[i][1] * qs[i + 1]
    return qs


def pick(values, index):
    out = jnp.zeros_like(values[0])
    for i, value in enumerate(values):
        out = jnp.where(index == i, value, out)
    return out


def kernel(sizes, clusters, cond_ref, label_ref, dens_ref, t_hbm, f_hbm, m_hbm, next_ref, force_ref,
           t_v, f_v, m_v, k_v, flux_v, hys, hyr, hzs, hzr, xm, ym, zm, xb, yb, zb, lab, cbuf,
           in_sem, hs_sem, hr_sem, relay_x, relay_z, *sems):
    nx, ny, nz = sizes
    me = {axis: lax.axis_index(axis) for axis in AXES}
    count = dict(zip(AXES, sizes))
    cz, cy, cx = 8, 16, 128
    lines = cz * cy

    def target(axes, index):
        ids = dict(me)
        for axis in reversed(axes):
            ids[axis] = lax.rem(index, count[axis])
            index = index // count[axis]
        return tuple(ids[axis] for axis in AXES)

    def place(axes):
        n, here = 1, 0
        for axis in axes:
            n, here = n * count[axis], here * count[axis] + me[axis]
        return n, here

    stages_c = [("gx", "gy")] if nx * ny <= 16 else [("gx",), ("gy",)]
    hyr[...] = jnp.zeros_like(hyr)
    hzr[...] = jnp.zeros_like(hzr)
    barrier = pltpu.get_barrier_semaphore()
    greeted = 0

    def greet(axes, index):
        pl.semaphore_signal(barrier, inc=1, device_id=target(axes, index), device_id_type=MESH)

    square = nx == 4
    partners_x = [me["gx"] + 1 - 2 * lax.rem(me["gx"], 2), lax.rem(me["gx"] + 2, nx)] if square else [
        lax.rem(me["gx"] + d, nx) for d in range(1, nx)]
    for index in partners_x:
        greet(("gx",), index)
    for d in range(1, ny):
        greet(("gy",), lax.rem(me["gy"] + d, ny))
    greeted = len(partners_x) + ny - 1
    below_z, above_z = me["gz"] > 0, me["gz"] < nz - 1
    near_z = ((below_z, lax.rem(me["gz"] + nz - 1, nz)), (above_z, lax.rem(me["gz"] + 1, nz)))
    line_z = nz <= 4
    if line_z:
        for has, index in near_z:
            pl.when(has)(functools.partial(greet, ("gz",), index))
        count_z = jnp.where(below_z, 1, 0) + jnp.where(above_z, 1, 0)
        greeted = greeted + count_z
    else:
        for d in range(1, nz):
            greet(("gz",), lax.rem(me["gz"] + d, nz))
        greeted += nz - 1
    ins = [pltpu.make_async_copy(s, d, in_sem.at[i])
           for i, (s, d) in enumerate(((m_hbm, m_v), (t_hbm, t_v), (f_hbm, f_v)))]
    for c in ins:
        c.start()

    finish = []

    class Gather:
        def __init__(self, buf, axes, ssem, rsem, edge=None):
            self.buf, self.axes, self.ssem, self.rsem, self.edge = buf, axes, ssem, rsem, edge
            self.n, self.here = place(axes)

        def copies(self, d, slot):
            def make(ref):
                return pltpu.make_async_remote_copy(
                    src_ref=ref, dst_ref=ref, send_sem=self.ssem.at[d - 1], recv_sem=self.rsem.at[slot],
                    device_id=target(self.axes, lax.rem(self.here + d, self.n)), device_id_type=MESH)
            if self.edge is None:
                return [(None, make(self.buf.at[slot]))]
            rows, offset = self.edge
            first, last = slot == 0, slot == self.n - 1
            return [(first, make(self.buf.at[slot, pl.ds(offset, rows)])),
                    (last, make(self.buf.at[slot, pl.ds(0, rows)])),
                    (jnp.logical_not(first | last), make(self.buf.at[slot]))]

        @staticmethod
        def do(has, action):
            if has is None:
                action()
            else:
                pl.when(has)(action)

        def start(self):
            for d in range(1, self.n):
                for has, c in self.copies(d, self.here):
                    self.do(has, c.start)
                    finish.append((has, c))

        def wait(self):
            for d in range(1, self.n):
                for has, c in self.copies(d, lax.rem(self.here + self.n - d, self.n)):
                    self.do(has, c.wait_recv)

    gathers = []
    specs = [(xm, ("gx",)), (ym, ("gy",)), (zm, ("gz",)), (xb, ("gx",)), (yb, ("gy",)), (zb, ("gz",)),
             (lab, ("gz",))]
    for i, (buf, axes) in enumerate(specs):
        edge = {2: (16, 32), 5: (24, 16)}.get(i)
        gathers.append(Gather(buf, axes, sems[2 * i], sems[2 * i + 1], edge))
    gxm, gym, gzm, gxb, gyb, gzb, glab = gathers

    rows8 = lax.broadcasted_iota(jnp.int32, (8, 128), 0)
    lanes8 = lax.broadcasted_iota(jnp.int32, (8, 128), 1)
    own_label = jnp.zeros((8, 128), jnp.float32)
    for t in range(8):
        own_label = jnp.where(rows8 == t, label_ref[0, t // 4, t % 4].astype(jnp.float32), own_label)
    lab[me["gz"]] = own_label

    ins[0].wait()
    material = m_v[...]
    k = jnp.zeros(material.shape, jnp.float32)
    for level in range(8):
        k = jnp.where(material == level, cond_ref[level], k)
    k_v[...] = k
    ins[1].wait()

    def yz(ref):
        return jnp.concatenate([ref[pl.ds(y, cz, stride=cy), :][None] for y in range(cy)], axis=0)

    k_yz, t_yz = yz(k_v), yz(t_v)
    k_zy, t_zy = k.reshape(cz, cy, cx), t_v[...].reshape(cz, cy, cx)
    for axis_k, axis_t, buf in ((k_yz, t_yz, hys), (k_zy, t_zy, hzs)):
        n = axis_k.shape[0]
        for side, at in ((0, 0), (1, n - 1)):
            buf[side, 0] = axis_k[at]
            buf[side, 1] = axis_t[at]

    pl.semaphore_wait(barrier, greeted)
    if square:
        pl.semaphore_signal(relay_x, inc=1, device_id=target(("gx",), partners_x[0]), device_id_type=MESH)

    halos = []
    for i, (axis, sbuf, rbuf) in enumerate((("gz", hzs, hzr), ("gy", hys, hyr))):
        n, here = count[axis], me[axis]
        for side in (0, 1):
            other = lax.rem(here + (1 if side else n - 1), n)
            c = pltpu.make_async_remote_copy(
                src_ref=sbuf.at[side], dst_ref=rbuf.at[1 - side], send_sem=hs_sem.at[2 * i + side],
                recv_sem=hr_sem.at[2 * i + 1 - side], device_id=target((axis,), other), device_id_type=MESH)
            r = pltpu.make_async_remote_copy(
                src_ref=sbuf.at[side], dst_ref=rbuf.at[side], send_sem=hs_sem.at[2 * i + side],
                recv_sem=hr_sem.at[2 * i + side], device_id=target((axis,), other), device_id_type=MESH)
            has = here < n - 1 if side else here > 0
            halos.append((has, c, r))
            pl.when(has)(c.start)
    k_x = k_yz.reshape(lines, cx).T
    t_x = t_yz.reshape(lines, cx).T

    a_x = half_face(k_x, LATERAL_RATE)
    a_y = half_face(k_yz, LATERAL_RATE)
    a_z = half_face(k_zy, VERTICAL_RATE)

    def ends(first, last, kk, rate):
        n = first.shape[0]
        return (last[n - 1:] + 1.0 / (rate * kk[n - 1:]), first[:1] + 1.0 / (rate * kk[:1]), first[n - 1:])

    def put3(buf, here, parts):
        for i, part in enumerate(parts):
            if part.ndim == 2:
                buf[here, i:i + 1] = part
            else:
                buf[here, i] = part[0]

    def get(buf, i, j):
        return buf[i, j:j + 1] if len(buf.shape) == 3 else buf[i, j][None]

    stages_x, inv_x, first_x, last_x = factor(a_x)
    put3(xm, me["gx"], ends(first_x, last_x, k_x, LATERAL_RATE))
    if square:
        pl.semaphore_wait(relay_x, 1)
    gxm.start()

    def inner_flux(a, t):
        flow = 2.0 * a * (t - down(t, 1))
        return up(flow, 1) - flow

    ins[2].wait()
    flux_x = inner_flux(a_x, t_x)
    flux_y = inner_flux(a_y, t_yz) + 0.5 * yz(f_v)
    flux_z = inner_flux(a_z, t_zy)

    for has, c, r in halos:
        pl.when(has)(r.wait_recv)
    if line_z:
        for has, index in near_z:
            pl.when(has)(functools.partial(pl.semaphore_signal, relay_z, inc=1, device_id=target(("gz",), index),
                                           device_id_type=MESH))

    def halo_flux(k_own, t_own, k_far, t_far, rate):
        return 2.0 * rate * k_own * k_far / (k_own + k_far) * (t_far - t_own)

    def with_halo(flux, kk, tt, buf, rate):
        n = flux.shape[0]
        low = halo_flux(kk[:1], tt[:1], buf[0, 0][None], buf[0, 1][None], rate)
        high = halo_flux(kk[n - 1:], tt[n - 1:], buf[1, 0][None], buf[1, 1][None], rate)
        return jnp.concatenate([flux[:1] + low, flux[1:n - 1], flux[n - 1:] + high], axis=0)

    flux_v[...] = with_halo(flux_z, k_zy, t_zy, hzr, VERTICAL_RATE).reshape(lines, cx)
    flux_y = with_halo(flux_y, k_yz, t_yz, hyr, LATERAL_RATE) + yz(flux_v)
    residual = flux_x + flux_y.reshape(lines, cx).T

    r_x = apply_stages(stages_x, inv_x, residual)
    put3(xb, me["gx"], (r_x[:1] + 2.0 * t_x[:1], r_x[cx - 1:] + 2.0 * t_x[cx - 1:]))
    gxb.start()

    stages_y, inv_y, first_y, last_y = factor(a_y)
    put3(ym, me["gy"], ends(first_y, last_y, k_yz, LATERAL_RATE))
    gym.start()
    stages_z, inv_z, first_z, last_z = factor(a_z)
    high_z, low_z, cross_z = ends(first_z, last_z, k_zy, VERTICAL_RATE)
    for i, part in enumerate((low_z, cross_z, high_z)):
        zm[me["gz"], i * cy:(i + 1) * cy] = part[0]
    if line_z:
        pl.semaphore_wait(relay_z, count_z)
    gzm.start()
    glab.start()
    gxm.wait()
    elim_x = chain_factor([tuple(get(xm, i, j) for j in range(3)) for i in range(nx)])
    gxb.wait()

    def join(buf, n, elim, r, first, last, here):
        if buf is zb:
            firsts, lasts = [zb[i, :cy][None] for i in range(n)], [zb[i, 24:40][None] for i in range(n)]
        else:
            firsts, lasts = [get(buf, i, 0) for i in range(n)], [get(buf, i, 1) for i in range(n)]
        qs = chain_flux(elim, firsts, lasts)
        return r + pick(qs, here - 1) * first - pick(qs, here) * last, qs

    step, _ = join(xb, nx, elim_x, r_x, first_x, last_x, me["gx"])
    r_y = apply_stages(stages_y, inv_y, step.T.reshape(cy, cz, cx))
    put3(yb, me["gy"], (r_y[:1], r_y[cy - 1:]))
    gyb.start()

    gym.wait()
    elim_y = chain_factor([tuple(get(ym, i, j) for j in range(3)) for i in range(ny)])
    gyb.wait()
    step, _ = join(yb, ny, elim_y, r_y, first_y, last_y, me["gy"])
    for y in range(cy):
        flux_v[pl.ds(y, cz, stride=cy), :] = step[y]
    rhs_z = flux_v[...].reshape(cz, cy, cx)
    r_z = apply_stages(stages_z, inv_z, rhs_z)
    zb[me["gz"], 0:cy] = r_z[0]
    zb[me["gz"], 24:40] = r_z[cz - 1]
    columns = jnp.sum(t_zy + rhs_z, axis=0)
    for i in range(cy // TY):
        zb[me["gz"], 16 + i:17 + i] = jnp.sum(columns[i * TY:(i + 1) * TY], axis=0, keepdims=True)
    gzb.start()

    gzm.wait()
    elim_z = chain_factor([tuple(zm[i, j * cy:(j + 1) * cy][None] for j in (2, 0, 1)) for i in range(nz)])
    glab.wait()
    width = cbuf.shape[-1] if len(cbuf.shape) == 3 else 128
    ids = lax.broadcasted_iota(jnp.int32, (8, width), 1).astype(jnp.float32)

    def onehot(labels):
        return jnp.concatenate([labels] * (width // 128), axis=1) == ids

    in_tile = lanes8 // TX == rows8 % 4
    gzb.wait()
    step, qs = join(zb, nz, elim_z, r_z, first_z, last_z, me["gz"])

    total = jnp.zeros((8, width), jnp.float32)
    for i in range(nz):
        cells = jnp.zeros((cy, cx), jnp.float32)
        if i > 0:
            cells = cells + qs[i - 1][0]
        if i < nz - 1:
            cells = cells - qs[i][0]
        upper = zb[i, 16:17] + jnp.sum(cells[:TY], axis=0, keepdims=True)
        lower = zb[i, 17:18] + jnp.sum(cells[TY:], axis=0, keepdims=True)
        tiles = jnp.where(in_tile, jnp.where(rows8 < 4, upper, lower), 0.0)
        sums = jnp.sum(tiles, axis=1, keepdims=True)
        total = total + jnp.where(onehot(lab[i]), sums, 0.0)
    total = jnp.sum(total, axis=0, keepdims=True)
    base = 0
    for j, axes in enumerate(stages_c):
        n, here = place(axes)
        part = Gather(cbuf.at[pl.ds(base, n)], axes, sems[14 + 2 * j], sems[15 + 2 * j])
        cbuf[base + here, 0:1] = total
        part.start()
        if j == 0:
            next_ref[...] = (t_zy + step).reshape(lines, cx)
        part.wait()
        total = cbuf[base, 0:1]
        for i in range(1, n):
            total = total + cbuf[base + i, 0:1]
        base += n

    mean = total / (4 * cz * TY * TX)
    leak = dens_ref[...] * jnp.exp(LEAK_SLOPE * mean[:, :clusters])
    power = jnp.sum(jnp.where(onehot(own_label)[:, :clusters], leak, 0.0), axis=1, keepdims=True)
    spread = jnp.where(in_tile, power, 0.0)
    upper = jnp.sum(spread[:4], axis=0, keepdims=True)
    lower = jnp.sum(spread[4:], axis=0, keepdims=True)
    rows16 = lax.broadcasted_iota(jnp.int32, (cy, cx), 0)
    layer = jnp.where(rows16 < TY, upper, lower)
    force_ref[...] = (f_v[...].reshape(cz, cy, cx) + layer[None]).reshape(lines, cx)

    for has, c, r in halos:
        pl.when(has)(c.wait_send)
    for has, c in finish:
        Gather.do(has, c.wait_send)


def per_device(sizes, thermal_field, forcing_per_step, substance_label, thermal_conductivities,
               patch_group_label, drain_power_density):
    nx, ny, nz = sizes
    shape = thermal_field.shape
    cz, cy, cx = shape
    lines = cz * cy
    clusters = drain_power_density.shape[0]
    width = -(-clusters // 128) * 128
    f32 = jnp.float32
    flat = lambda v: v.reshape(lines, cx)
    vm = lambda *s: pltpu.VMEM(s, f32)
    dma = pltpu.SemaphoreType.DMA
    small = nx * ny <= 16
    csizes = [nx * ny] if small else [nx, ny]
    sems = []
    for n in [nx, ny, nz, nx, ny, nz, nz] + csizes:
        sems += [dma((max(n - 1, 1),)), dma((n,))]
    any_spec = pl.BlockSpec(memory_space=pl.ANY)
    smem = pl.BlockSpec(memory_space=pltpu.SMEM)
    new, force = pl.pallas_call(
        functools.partial(kernel, sizes, clusters),
        out_shape=[pltpu.VMEM((lines, cx), f32)] * 2,
        in_specs=[smem, smem, pl.BlockSpec(memory_space=pltpu.VMEM), any_spec, any_spec, any_spec],
        out_specs=[pl.BlockSpec(memory_space=pltpu.VMEM)] * 2,
        scratch_shapes=[
            vm(lines, cx), vm(lines, cx), pltpu.VMEM((lines, cx), jnp.int32), vm(lines, cx), vm(lines, cx),
            vm(2, 2, cz, cx), vm(2, 2, cz, cx), vm(2, 2, cy, cx), vm(2, 2, cy, cx),
            vm(nx, 8, lines), vm(ny, 3, cz, cx), vm(nz, 48, cx),
            vm(nx, 8, lines), vm(ny, 2, cz, cx), vm(nz, 40, cx),
            vm(nz, 8, 128), vm(sum(csizes), 1, width),
            dma((3,)), dma((4,)), dma((4,)), pltpu.SemaphoreType.REGULAR, pltpu.SemaphoreType.REGULAR,
        ] + sems,
        compiler_params=pltpu.CompilerParams(collective_id=0, has_side_effects=True),
    )(thermal_conductivities, patch_group_label, drain_power_density.reshape(1, clusters),
      flat(thermal_field), flat(forcing_per_step), flat(substance_label))
    return new.reshape(shape), force.reshape(shape)


def solution(mesh):
    block = P("gz", "gy", "gx")
    return jax.shard_map(
        functools.partial(per_device, tuple(mesh.shape[axis] for axis in AXES)),
        mesh=mesh, in_specs=(block, block, block, P(), block, P()), out_specs=(block, block), check_vma=False,
    )
```

```python
import functools

import jax
import jax.numpy as jnp
from jax import lax
from jax.experimental import pallas as pl
from jax.experimental.pallas import tpu as pltpu
from jax.sharding import PartitionSpec as P

TX = 32
TY = 8
LATERAL_RATE = 100.0
VERTICAL_RATE = 400.0
LEAK_SLOPE = 0.5
AXES = ("gx", "gy", "gz")
MESH = pl.DeviceIdType.MESH


def down(v, s):
    n = v.shape[0]
    s = s % n
    if s == 0:
        return v
    if v.ndim == 2 and s % 8:
        return pltpu.roll(v, s, 0)
    return jnp.concatenate([v[n - s:], v[: n - s]], axis=0)


def up(v, s):
    return down(v, v.shape[0] - s % v.shape[0])


def half_face(k, rate):
    below = down(k, 1)
    face = rate * k * below / (k + below)
    return jnp.where(lax.broadcasted_iota(jnp.int32, k.shape, 0) == 0, 0.0, face)


def factor(a):
    n = a.shape[0]
    rows = lax.broadcasted_iota(jnp.int32, a.shape, 0)
    first = jnp.where(rows == 0, 1.0, 0.0)
    last = jnp.where(rows == n - 1, 1.0, 0.0)
    excess = jnp.ones_like(a)
    b = up(a, 1)
    stages = []
    s = 1
    while s < n:
        inv = 1.0 / (excess + a + b)
        fd = a * down(inv, s)
        fu = b * up(inv, s)
        stages.append((s, fd, fu))
        excess = excess + fd * down(excess, s) + fu * up(excess, s)
        first = first + fd * down(first, s) + fu * up(first, s)
        last = last + fd * down(last, s) + fu * up(last, s)
        a = fd * down(a, s)
        b = up(a, 2 * s)
        s *= 2
    inv = 1.0 / excess
    return stages, inv, first * inv, last * inv


def apply_stages(stages, inv, r):
    for s, fd, fu in stages:
        r = r + fd * down(r, s) + fu * up(r, s)
    return r * inv


def chain_factor(mats):
    out = []
    slope = None
    for i in range(len(mats) - 1):
        den = mats[i][0] + mats[i + 1][1]
        if slope is not None:
            den = den - mats[i][2] * slope
        inv = 1.0 / den
        slope = mats[i + 1][2] * inv if i < len(mats) - 2 else None
        out.append((inv, slope, mats[i][2]))
    return out


def chain_flux(elim, firsts, lasts):
    ys = []
    for i, (inv, _, cross) in enumerate(elim):
        rhs = lasts[i] - firsts[i + 1]
        if i:
            rhs = rhs + cross * ys[-1]
        ys.append(rhs * inv)
    qs = [None] * len(ys)
    for i in reversed(range(len(ys))):
        qs[i] = ys[i] if i == len(ys) - 1 else ys[i] + elim[i][1] * qs[i + 1]
    return qs


def pick(values, index):
    out = jnp.zeros_like(values[0])
    for i, value in enumerate(values):
        out = jnp.where(index == i, value, out)
    return out


def kernel(sizes, clusters, cond_hbm, label_hbm, dens_hbm, t_hbm, f_hbm, m_hbm, next_ref, force_ref,
           cond_ref, label_ref, dens_ref, t_v, f_v, m_v, k_v, flux_v, hys, hyr, hzs, hzr, xm, ym, zm, xb, yb, zb, lab, cbuf,
           in_sem, hs_sem, hr_sem, relay_x, relay_z, *sems):
    nx, ny, nz = sizes
    me = {axis: lax.axis_index(axis) for axis in AXES}
    count = dict(zip(AXES, sizes))
    cz, cy, cx = 8, 16, 128
    lines = cz * cy

    def target(axes, index):
        ids = dict(me)
        for axis in reversed(axes):
            ids[axis] = lax.rem(index, count[axis])
            index = index // count[axis]
        return tuple(ids[axis] for axis in AXES)

    def place(axes):
        n, here = 1, 0
        for axis in axes:
            n, here = n * count[axis], here * count[axis] + me[axis]
        return n, here

    stages_c = [("gx", "gy")] if nx * ny <= 16 else [("gx",), ("gy",)]
    hyr[...] = jnp.zeros_like(hyr)
    hzr[...] = jnp.zeros_like(hzr)
    barrier = pltpu.get_barrier_semaphore()
    greeted = 0

    def greet(axes, index):
        pl.semaphore_signal(barrier, inc=1, device_id=target(axes, index), device_id_type=MESH)

    square = nx == 4
    partners_x = [me["gx"] + 1 - 2 * lax.rem(me["gx"], 2), lax.rem(me["gx"] + 2, nx)] if square else [
        lax.rem(me["gx"] + d, nx) for d in range(1, nx)]
    for index in partners_x:
        greet(("gx",), index)
    for d in range(1, ny):
        greet(("gy",), lax.rem(me["gy"] + d, ny))
    greeted = len(partners_x) + ny - 1
    below_z, above_z = me["gz"] > 0, me["gz"] < nz - 1
    near_z = ((below_z, lax.rem(me["gz"] + nz - 1, nz)), (above_z, lax.rem(me["gz"] + 1, nz)))
    line_z = nz <= 4
    if line_z:
        for has, index in near_z:
            pl.when(has)(functools.partial(greet, ("gz",), index))
        count_z = jnp.where(below_z, 1, 0) + jnp.where(above_z, 1, 0)
        greeted = greeted + count_z
    else:
        for d in range(1, nz):
            greet(("gz",), lax.rem(me["gz"] + d, nz))
        greeted += nz - 1
    ins = [pltpu.make_async_copy(s, d, in_sem.at[i])
           for i, (s, d) in enumerate((
               (m_hbm, m_v), (t_hbm, t_v), (f_hbm, f_v), (cond_hbm, cond_ref), (label_hbm, label_ref), (dens_hbm, dens_ref)))]
    for i in (3, 0, 1, 4, 2, 5):
        ins[i].start()

    finish = []

    class Gather:
        def __init__(self, buf, axes, ssem, rsem, edge=None):
            self.buf, self.axes, self.ssem, self.rsem, self.edge = buf, axes, ssem, rsem, edge
            self.n, self.here = place(axes)

        def copies(self, d, slot):
            def make(ref):
                return pltpu.make_async_remote_copy(
                    src_ref=ref, dst_ref=ref, send_sem=self.ssem.at[d - 1], recv_sem=self.rsem.at[slot],
                    device_id=target(self.axes, lax.rem(self.here + d, self.n)), device_id_type=MESH)
            if self.edge is None:
                return [(None, make(self.buf.at[slot]))]
            rows, offset = self.edge
            first, last = slot == 0, slot == self.n - 1
            return [(first, make(self.buf.at[slot, pl.ds(offset, rows)])),
                    (last, make(self.buf.at[slot, pl.ds(0, rows)])),
                    (jnp.logical_not(first | last), make(self.buf.at[slot]))]

        @staticmethod
        def do(has, action):
            if has is None:
                action()
            else:
                pl.when(has)(action)

        def start(self):
            for d in range(1, self.n):
                for has, c in self.copies(d, self.here):
                    self.do(has, c.start)
                    finish.append((has, c))

        def wait(self):
            for d in range(1, self.n):
                for has, c in self.copies(d, lax.rem(self.here + self.n - d, self.n)):
                    self.do(has, c.wait_recv)

    gathers = []
    specs = [(xm, ("gx",)), (ym, ("gy",)), (zm, ("gz",)), (xb, ("gx",)), (yb, ("gy",)), (zb, ("gz",)),
             (lab, ("gz",))]
    for i, (buf, axes) in enumerate(specs):
        edge = {2: (16, 32), 5: (24, 16)}.get(i)
        gathers.append(Gather(buf, axes, sems[2 * i], sems[2 * i + 1], edge))
    gxm, gym, gzm, gxb, gyb, gzb, glab = gathers

    ins[3].wait()
    ins[0].wait()
    material = m_v[...]
    k = jnp.zeros(material.shape, jnp.float32)
    for level in range(8):
        k = jnp.where(material == level, cond_ref[level], k)
    k_v[...] = k
    ins[1].wait()

    def yz(ref):
        return jnp.concatenate([ref[pl.ds(y, cz, stride=cy), :][None] for y in range(cy)], axis=0)

    k_yz, t_yz = yz(k_v), yz(t_v)
    k_zy, t_zy = k.reshape(cz, cy, cx), t_v[...].reshape(cz, cy, cx)
    for axis_k, axis_t, buf in ((k_yz, t_yz, hys), (k_zy, t_zy, hzs)):
        n = axis_k.shape[0]
        for side, at in ((0, 0), (1, n - 1)):
            buf[side, 0] = axis_k[at]
            buf[side, 1] = axis_t[at]

    pl.semaphore_wait(barrier, greeted)
    if square:
        pl.semaphore_signal(relay_x, inc=1, device_id=target(("gx",), partners_x[0]), device_id_type=MESH)

    halos = []
    for i, (axis, sbuf, rbuf) in enumerate((("gz", hzs, hzr), ("gy", hys, hyr))):
        n, here = count[axis], me[axis]
        for side in (0, 1):
            other = lax.rem(here + (1 if side else n - 1), n)
            c = pltpu.make_async_remote_copy(
                src_ref=sbuf.at[side], dst_ref=rbuf.at[1 - side], send_sem=hs_sem.at[2 * i + side],
                recv_sem=hr_sem.at[2 * i + 1 - side], device_id=target((axis,), other), device_id_type=MESH)
            r = pltpu.make_async_remote_copy(
                src_ref=sbuf.at[side], dst_ref=rbuf.at[side], send_sem=hs_sem.at[2 * i + side],
                recv_sem=hr_sem.at[2 * i + side], device_id=target((axis,), other), device_id_type=MESH)
            has = here < n - 1 if side else here > 0
            halos.append((has, c, r))
            pl.when(has)(c.start)
    ins[4].wait()
    rows8 = lax.broadcasted_iota(jnp.int32, (8, 128), 0)
    lanes8 = lax.broadcasted_iota(jnp.int32, (8, 128), 1)
    own_label = jnp.zeros((8, 128), jnp.float32)
    for t in range(8):
        own_label = jnp.where(rows8 == t, label_ref[0, t // 4, t % 4].astype(jnp.float32), own_label)
    lab[me["gz"]] = own_label

    k_x = k_yz.reshape(lines, cx).T
    t_x = t_yz.reshape(lines, cx).T

    a_x = half_face(k_x, LATERAL_RATE)
    a_y = half_face(k_yz, LATERAL_RATE)
    a_z = half_face(k_zy, VERTICAL_RATE)

    def ends(first, last, kk, rate):
        n = first.shape[0]
        return (last[n - 1:] + 1.0 / (rate * kk[n - 1:]), first[:1] + 1.0 / (rate * kk[:1]), first[n - 1:])

    def put3(buf, here, parts):
        for i, part in enumerate(parts):
            if part.ndim == 2:
                buf[here, i:i + 1] = part
            else:
                buf[here, i] = part[0]

    def get(buf, i, j):
        return buf[i, j:j + 1] if len(buf.shape) == 3 else buf[i, j][None]

    stages_x, inv_x, first_x, last_x = factor(a_x)
    put3(xm, me["gx"], ends(first_x, last_x, k_x, LATERAL_RATE))
    if square:
        pl.semaphore_wait(relay_x, 1)
    gxm.start()

    def inner_flux(a, t):
        flow = 2.0 * a * (t - down(t, 1))
        return up(flow, 1) - flow

    ins[2].wait()
    ins[5].wait()
    flux_x = inner_flux(a_x, t_x)
    flux_y = inner_flux(a_y, t_yz) + 0.5 * yz(f_v)
    flux_z = inner_flux(a_z, t_zy)

    stages_z, inv_z, first_z, last_z = factor(a_z)
    high_z, low_z, cross_z = ends(first_z, last_z, k_zy, VERTICAL_RATE)
    for i, part in enumerate((low_z, cross_z, high_z)):
        zm[me["gz"], i * cy:(i + 1) * cy] = part[0]
    stages_y, inv_y, first_y, last_y = factor(a_y)
    put3(ym, me["gy"], ends(first_y, last_y, k_yz, LATERAL_RATE))
    gym.start()
    for has, c, r in halos:
        pl.when(has)(r.wait_recv)
    if line_z:
        for has, index in near_z:
            pl.when(has)(functools.partial(pl.semaphore_signal, relay_z, inc=1, device_id=target(("gz",), index),
                                           device_id_type=MESH))

    def halo_flux(k_own, t_own, k_far, t_far, rate):
        return 2.0 * rate * k_own * k_far / (k_own + k_far) * (t_far - t_own)

    def with_halo(flux, kk, tt, buf, rate):
        n = flux.shape[0]
        low = halo_flux(kk[:1], tt[:1], buf[0, 0][None], buf[0, 1][None], rate)
        high = halo_flux(kk[n - 1:], tt[n - 1:], buf[1, 0][None], buf[1, 1][None], rate)
        return jnp.concatenate([flux[:1] + low, flux[1:n - 1], flux[n - 1:] + high], axis=0)

    flux_v[...] = with_halo(flux_z, k_zy, t_zy, hzr, VERTICAL_RATE).reshape(lines, cx)
    flux_y = with_halo(flux_y, k_yz, t_yz, hyr, LATERAL_RATE) + yz(flux_v)
    residual = flux_x + flux_y.reshape(lines, cx).T

    r_x = apply_stages(stages_x, inv_x, residual)
    put3(xb, me["gx"], (r_x[:1] + 2.0 * t_x[:1], r_x[cx - 1:] + 2.0 * t_x[cx - 1:]))
    gxb.start()

    if line_z:
        pl.semaphore_wait(relay_z, count_z)
    gzm.start()
    glab.start()
    gxm.wait()
    elim_x = chain_factor([tuple(get(xm, i, j) for j in range(3)) for i in range(nx)])
    gxb.wait()

    def join(buf, n, elim, r, first, last, here):
        if buf is zb:
            firsts, lasts = [zb[i, :cy][None] for i in range(n)], [zb[i, 24:40][None] for i in range(n)]
        else:
            firsts, lasts = [get(buf, i, 0) for i in range(n)], [get(buf, i, 1) for i in range(n)]
        qs = chain_flux(elim, firsts, lasts)
        return r + pick(qs, here - 1) * first - pick(qs, here) * last, qs

    step, _ = join(xb, nx, elim_x, r_x, first_x, last_x, me["gx"])
    r_y = apply_stages(stages_y, inv_y, step.T.reshape(cy, cz, cx))
    put3(yb, me["gy"], (r_y[:1], r_y[cy - 1:]))
    gyb.start()

    gym.wait()
    elim_y = chain_factor([tuple(get(ym, i, j) for j in range(3)) for i in range(ny)])
    gyb.wait()
    step, _ = join(yb, ny, elim_y, r_y, first_y, last_y, me["gy"])
    for y in range(cy):
        flux_v[pl.ds(y, cz, stride=cy), :] = step[y]
    rhs_z = flux_v[...].reshape(cz, cy, cx)
    r_z = apply_stages(stages_z, inv_z, rhs_z)
    zb[me["gz"], 0:cy] = r_z[0]
    zb[me["gz"], 24:40] = r_z[cz - 1]
    columns = jnp.sum(t_zy + rhs_z, axis=0)
    for i in range(cy // TY):
        zb[me["gz"], 16 + i:17 + i] = jnp.sum(columns[i * TY:(i + 1) * TY], axis=0, keepdims=True)
    gzb.start()

    gzm.wait()
    elim_z = chain_factor([tuple(zm[i, j * cy:(j + 1) * cy][None] for j in (2, 0, 1)) for i in range(nz)])
    glab.wait()
    width = cbuf.shape[-1] if len(cbuf.shape) == 3 else 128
    ids = lax.broadcasted_iota(jnp.int32, (8, width), 1).astype(jnp.float32)

    def onehot(labels):
        return jnp.concatenate([labels] * (width // 128), axis=1) == ids

    in_tile = lanes8 // TX == rows8 % 4
    gzb.wait()
    step, qs = join(zb, nz, elim_z, r_z, first_z, last_z, me["gz"])

    total = jnp.zeros((8, width), jnp.float32)
    for i in range(nz):
        cells = jnp.zeros((cy, cx), jnp.float32)
        if i > 0:
            cells = cells + qs[i - 1][0]
        if i < nz - 1:
            cells = cells - qs[i][0]
        upper = zb[i, 16:17] + jnp.sum(cells[:TY], axis=0, keepdims=True)
        lower = zb[i, 17:18] + jnp.sum(cells[TY:], axis=0, keepdims=True)
        tiles = jnp.where(in_tile, jnp.where(rows8 < 4, upper, lower), 0.0)
        sums = jnp.sum(tiles, axis=1, keepdims=True)
        total = total + jnp.where(onehot(lab[i]), sums, 0.0)
    total = jnp.sum(total, axis=0, keepdims=True)
    base = 0
    for j, axes in enumerate(stages_c):
        n, here = place(axes)
        part = Gather(cbuf.at[pl.ds(base, n)], axes, sems[14 + 2 * j], sems[15 + 2 * j])
        cbuf[base + here, 0:1] = total
        part.start()
        if j == 0:
            next_ref[...] = (t_zy + step).reshape(lines, cx)
        part.wait()
        total = cbuf[base, 0:1]
        for i in range(1, n):
            total = total + cbuf[base + i, 0:1]
        base += n

    mean = total / (4 * cz * TY * TX)
    leak = dens_ref[...] * jnp.exp(LEAK_SLOPE * mean[:, :clusters])
    power = jnp.sum(jnp.where(onehot(own_label)[:, :clusters], leak, 0.0), axis=1, keepdims=True)
    spread = jnp.where(in_tile, power, 0.0)
    upper = jnp.sum(spread[:4], axis=0, keepdims=True)
    lower = jnp.sum(spread[4:], axis=0, keepdims=True)
    rows16 = lax.broadcasted_iota(jnp.int32, (cy, cx), 0)
    layer = jnp.where(rows16 < TY, upper, lower)
    force_ref[...] = (f_v[...].reshape(cz, cy, cx) + layer[None]).reshape(lines, cx)

    for has, c, r in halos:
        pl.when(has)(c.wait_send)
    for has, c in finish:
        Gather.do(has, c.wait_send)


def per_device(sizes, thermal_field, forcing_per_step, substance_label, thermal_conductivities,
               patch_group_label, drain_power_density):
    nx, ny, nz = sizes
    shape = thermal_field.shape
    cz, cy, cx = shape
    lines = cz * cy
    clusters = drain_power_density.shape[0]
    width = -(-clusters // 128) * 128
    f32 = jnp.float32
    flat = lambda v: v.reshape(lines, cx)
    vm = lambda *s: pltpu.VMEM(s, f32)
    dma = pltpu.SemaphoreType.DMA
    small = nx * ny <= 16
    csizes = [nx * ny] if small else [nx, ny]
    sems = []
    for n in [nx, ny, nz, nx, ny, nz, nz] + csizes:
        sems += [dma((max(n - 1, 1),)), dma((n,))]
    any_spec = pl.BlockSpec(memory_space=pl.ANY)
    new, force = pl.pallas_call(
        functools.partial(kernel, sizes, clusters),
        out_shape=[pltpu.VMEM((lines, cx), f32)] * 2,
        in_specs=[any_spec] * 6,
        out_specs=[pl.BlockSpec(memory_space=pltpu.VMEM)] * 2,
        scratch_shapes=[
            pltpu.SMEM(thermal_conductivities.shape, f32), pltpu.SMEM(patch_group_label.shape, jnp.int32),
            vm(1, clusters),
            vm(lines, cx), vm(lines, cx), pltpu.VMEM((lines, cx), jnp.int32), vm(lines, cx), vm(lines, cx),
            vm(2, 2, cz, cx), vm(2, 2, cz, cx), vm(2, 2, cy, cx), vm(2, 2, cy, cx),
            vm(nx, 8, lines), vm(ny, 3, cz, cx), vm(nz, 48, cx),
            vm(nx, 8, lines), vm(ny, 2, cz, cx), vm(nz, 40, cx),
            vm(nz, 8, 128), vm(sum(csizes), 1, width),
            dma((6,)), dma((4,)), dma((4,)), pltpu.SemaphoreType.REGULAR, pltpu.SemaphoreType.REGULAR,
        ] + sems,
        compiler_params=pltpu.CompilerParams(collective_id=0, has_side_effects=True),
    )(thermal_conductivities, patch_group_label, drain_power_density.reshape(1, clusters),
      flat(thermal_field), flat(forcing_per_step), flat(substance_label))
    return new.reshape(shape), force.reshape(shape)


def solution(mesh):
    block = P("gz", "gy", "gx")
    return jax.shard_map(
        functools.partial(per_device, tuple(mesh.shape[axis] for axis in AXES)),
        mesh=mesh, in_specs=(block, block, block, P(), block, P()), out_specs=(block, block), check_vma=False,
    )
```

```python
import functools

import jax
import jax.numpy as jnp
from jax import lax
from jax.experimental import pallas as pl
from jax.experimental.pallas import tpu as pltpu
from jax.sharding import PartitionSpec as P

TX = 32
TY = 8
LATERAL_RATE = 100.0
VERTICAL_RATE = 400.0
LEAK_SLOPE = 0.5
AXES = ("gx", "gy", "gz")
MESH = pl.DeviceIdType.MESH


def down(v, s):
    n = v.shape[0]
    s = s % n
    if s == 0:
        return v
    if v.ndim == 2 and s % 8:
        return pltpu.roll(v, s, 0)
    return jnp.concatenate([v[n - s:], v[: n - s]], axis=0)


def up(v, s):
    return down(v, v.shape[0] - s % v.shape[0])


def half_face(k, rate):
    below = down(k, 1)
    face = rate * k * below / (k + below)
    return jnp.where(lax.broadcasted_iota(jnp.int32, k.shape, 0) == 0, 0.0, face)


def factor(a):
    n = a.shape[0]
    rows = lax.broadcasted_iota(jnp.int32, a.shape, 0)
    first = jnp.where(rows == 0, 1.0, 0.0)
    last = jnp.where(rows == n - 1, 1.0, 0.0)
    excess = jnp.ones_like(a)
    b = up(a, 1)
    stages = []
    s = 1
    while s < n:
        inv = 1.0 / (excess + a + b)
        fd = a * down(inv, s)
        fu = b * up(inv, s)
        stages.append((s, fd, fu))
        excess = excess + fd * down(excess, s) + fu * up(excess, s)
        first = first + fd * down(first, s) + fu * up(first, s)
        last = last + fd * down(last, s) + fu * up(last, s)
        a = fd * down(a, s)
        b = up(a, 2 * s)
        s *= 2
    inv = 1.0 / excess
    return stages, inv, first * inv, last * inv


def apply_stages(stages, inv, r):
    for s, fd, fu in stages:
        r = r + fd * down(r, s) + fu * up(r, s)
    return r * inv


def chain_factor(mats):
    out = []
    slope = None
    for i in range(len(mats) - 1):
        den = mats[i][0] + mats[i + 1][1]
        if slope is not None:
            den = den - mats[i][2] * slope
        inv = 1.0 / den
        slope = mats[i + 1][2] * inv if i < len(mats) - 2 else None
        out.append((inv, slope, mats[i][2]))
    return out


def chain_flux(elim, firsts, lasts):
    ys = []
    for i, (inv, _, cross) in enumerate(elim):
        rhs = lasts[i] - firsts[i + 1]
        if i:
            rhs = rhs + cross * ys[-1]
        ys.append(rhs * inv)
    qs = [None] * len(ys)
    for i in reversed(range(len(ys))):
        qs[i] = ys[i] if i == len(ys) - 1 else ys[i] + elim[i][1] * qs[i + 1]
    return qs


def pick(values, index):
    out = jnp.zeros_like(values[0])
    for i, value in enumerate(values):
        out = jnp.where(index == i, value, out)
    return out


def kernel(sizes, clusters, cond_hbm, label_hbm, dens_hbm, t_hbm, f_hbm, m_hbm, next_ref, force_ref,
           cond_ref, label_ref, dens_ref, t_v, f_v, m_v, k_v, flux_v, hys, hyr, hzs, hzr, xm, ym, zm, xb, yb, zb, lab, cbuf,
           in_sem, hs_sem, hr_sem, relay_x, relay_z, *sems):
    nx, ny, nz = sizes
    me = {axis: lax.axis_index(axis) for axis in AXES}
    count = dict(zip(AXES, sizes))
    cz, cy, cx = 8, 16, 128
    lines = cz * cy

    def target(axes, index):
        ids = dict(me)
        for axis in reversed(axes):
            ids[axis] = lax.rem(index, count[axis])
            index = index // count[axis]
        return tuple(ids[axis] for axis in AXES)

    def place(axes):
        n, here = 1, 0
        for axis in axes:
            n, here = n * count[axis], here * count[axis] + me[axis]
        return n, here

    stages_c = [("gx", "gy")] if nx * ny <= 16 else [("gx",), ("gy",)]
    hyr[...] = jnp.zeros_like(hyr)
    hzr[...] = jnp.zeros_like(hzr)
    barrier = pltpu.get_barrier_semaphore()
    greeted = 0

    def greet(axes, index):
        pl.semaphore_signal(barrier, inc=1, device_id=target(axes, index), device_id_type=MESH)

    square = nx == 4
    partners_x = [me["gx"] + 1 - 2 * lax.rem(me["gx"], 2), lax.rem(me["gx"] + 2, nx)] if square else [
        lax.rem(me["gx"] + d, nx) for d in range(1, nx)]
    for index in partners_x:
        greet(("gx",), index)
    for d in range(1, ny):
        greet(("gy",), lax.rem(me["gy"] + d, ny))
    greeted = len(partners_x) + ny - 1
    below_z, above_z = me["gz"] > 0, me["gz"] < nz - 1
    near_z = ((below_z, lax.rem(me["gz"] + nz - 1, nz)), (above_z, lax.rem(me["gz"] + 1, nz)))
    line_z = nz <= 4
    if line_z:
        for has, index in near_z:
            pl.when(has)(functools.partial(greet, ("gz",), index))
        count_z = jnp.where(below_z, 1, 0) + jnp.where(above_z, 1, 0)
        greeted = greeted + count_z
    else:
        for d in range(1, nz):
            greet(("gz",), lax.rem(me["gz"] + d, nz))
        greeted += nz - 1
    ins = [pltpu.make_async_copy(s, d, in_sem.at[i])
           for i, (s, d) in enumerate((
               (m_hbm, m_v), (t_hbm, t_v), (f_hbm, f_v), (cond_hbm, cond_ref), (label_hbm, label_ref), (dens_hbm, dens_ref)))]
    for i in (3, 0, 1, 4, 2, 5):
        ins[i].start()

    finish = []

    class Gather:
        def __init__(self, buf, axes, ssem, rsem, edge=None):
            self.buf, self.axes, self.ssem, self.rsem, self.edge = buf, axes, ssem, rsem, edge
            self.n, self.here = place(axes)

        def copies(self, d, slot):
            step = jnp.where(2 * self.here < self.n, self.n - d, d)

            def make(ref):
                return pltpu.make_async_remote_copy(
                    src_ref=ref, dst_ref=ref, send_sem=self.ssem.at[d - 1], recv_sem=self.rsem.at[slot],
                    device_id=target(self.axes, lax.rem(self.here + step, self.n)), device_id_type=MESH)
            if self.edge is None:
                return [(None, make(self.buf.at[slot]))]
            rows, offset = self.edge
            first, last = slot == 0, slot == self.n - 1
            return [(first, make(self.buf.at[slot, pl.ds(offset, rows)])),
                    (last, make(self.buf.at[slot, pl.ds(0, rows)])),
                    (jnp.logical_not(first | last), make(self.buf.at[slot]))]

        @staticmethod
        def do(has, action):
            if has is None:
                action()
            else:
                pl.when(has)(action)

        def start(self):
            for d in range(1, self.n):
                for has, c in self.copies(d, self.here):
                    self.do(has, c.start)
                    finish.append((has, c))

        def wait(self):
            for d in range(1, self.n):
                for has, c in self.copies(d, lax.rem(self.here + self.n - d, self.n)):
                    self.do(has, c.wait_recv)

    gathers = []
    specs = [(xm, ("gx",)), (ym, ("gy",)), (zm, ("gz",)), (xb, ("gx",)), (yb, ("gy",)), (zb, ("gz",)),
             (lab, ("gz",))]
    for i, (buf, axes) in enumerate(specs):
        edge = {2: (16, 32), 5: (24, 16)}.get(i)
        gathers.append(Gather(buf, axes, sems[2 * i], sems[2 * i + 1], edge))
    gxm, gym, gzm, gxb, gyb, gzb, glab = gathers

    ins[3].wait()
    ins[0].wait()
    material = m_v[...]
    k = jnp.zeros(material.shape, jnp.float32)
    for level in range(8):
        k = jnp.where(material == level, cond_ref[level], k)
    k_v[...] = k
    ins[1].wait()

    def yz(ref):
        return jnp.concatenate([ref[pl.ds(y, cz, stride=cy), :][None] for y in range(cy)], axis=0)

    k_yz, t_yz = yz(k_v), yz(t_v)
    k_zy, t_zy = k.reshape(cz, cy, cx), t_v[...].reshape(cz, cy, cx)
    for axis_k, axis_t, buf in ((k_yz, t_yz, hys), (k_zy, t_zy, hzs)):
        n = axis_k.shape[0]
        for side, at in ((0, 0), (1, n - 1)):
            buf[side, 0] = axis_k[at]
            buf[side, 1] = axis_t[at]

    pl.semaphore_wait(barrier, greeted)
    if square:
        pl.semaphore_signal(relay_x, inc=1, device_id=target(("gx",), partners_x[0]), device_id_type=MESH)

    halos = []
    for i, (axis, sbuf, rbuf) in enumerate((("gz", hzs, hzr), ("gy", hys, hyr))):
        n, here = count[axis], me[axis]
        for side in (0, 1):
            other = lax.rem(here + (1 if side else n - 1), n)
            c = pltpu.make_async_remote_copy(
                src_ref=sbuf.at[side], dst_ref=rbuf.at[1 - side], send_sem=hs_sem.at[2 * i + side],
                recv_sem=hr_sem.at[2 * i + 1 - side], device_id=target((axis,), other), device_id_type=MESH)
            r = pltpu.make_async_remote_copy(
                src_ref=sbuf.at[side], dst_ref=rbuf.at[side], send_sem=hs_sem.at[2 * i + side],
                recv_sem=hr_sem.at[2 * i + side], device_id=target((axis,), other), device_id_type=MESH)
            has = here < n - 1 if side else here > 0
            halos.append((has, c, r))
            pl.when(has)(c.start)
    ins[4].wait()
    rows8 = lax.broadcasted_iota(jnp.int32, (8, 128), 0)
    lanes8 = lax.broadcasted_iota(jnp.int32, (8, 128), 1)
    own_label = jnp.zeros((8, 128), jnp.float32)
    for t in range(8):
        own_label = jnp.where(rows8 == t, label_ref[0, t // 4, t % 4].astype(jnp.float32), own_label)
    lab[me["gz"]] = own_label

    k_x = k_yz.reshape(lines, cx).T
    t_x = t_yz.reshape(lines, cx).T

    a_x = half_face(k_x, LATERAL_RATE)
    a_y = half_face(k_yz, LATERAL_RATE)
    a_z = half_face(k_zy, VERTICAL_RATE)

    def ends(first, last, kk, rate):
        n = first.shape[0]
        return (last[n - 1:] + 1.0 / (rate * kk[n - 1:]), first[:1] + 1.0 / (rate * kk[:1]), first[n - 1:])

    def put3(buf, here, parts):
        for i, part in enumerate(parts):
            if part.ndim == 2:
                buf[here, i:i + 1] = part
            else:
                buf[here, i] = part[0]

    def get(buf, i, j):
        return buf[i, j:j + 1] if len(buf.shape) == 3 else buf[i, j][None]

    stages_x, inv_x, first_x, last_x = factor(a_x)
    put3(xm, me["gx"], ends(first_x, last_x, k_x, LATERAL_RATE))
    if square:
        pl.semaphore_wait(relay_x, 1)
    gxm.start()

    def inner_flux(a, t):
        flow = 2.0 * a * (t - down(t, 1))
        return up(flow, 1) - flow

    ins[2].wait()
    ins[5].wait()
    flux_x = inner_flux(a_x, t_x)
    flux_y = inner_flux(a_y, t_yz) + 0.5 * yz(f_v)
    flux_z = inner_flux(a_z, t_zy)

    stages_z, inv_z, first_z, last_z = factor(a_z)
    high_z, low_z, cross_z = ends(first_z, last_z, k_zy, VERTICAL_RATE)
    for i, part in enumerate((low_z, cross_z, high_z)):
        zm[me["gz"], i * cy:(i + 1) * cy] = part[0]
    stages_y, inv_y, first_y, last_y = factor(a_y)
    put3(ym, me["gy"], ends(first_y, last_y, k_yz, LATERAL_RATE))
    gym.start()
    for has, c, r in halos:
        pl.when(has)(r.wait_recv)
    if line_z:
        for has, index in near_z:
            pl.when(has)(functools.partial(pl.semaphore_signal, relay_z, inc=1, device_id=target(("gz",), index),
                                           device_id_type=MESH))

    def halo_flux(k_own, t_own, k_far, t_far, rate):
        return 2.0 * rate * k_own * k_far / (k_own + k_far) * (t_far - t_own)

    def with_halo(flux, kk, tt, buf, rate):
        n = flux.shape[0]
        low = halo_flux(kk[:1], tt[:1], buf[0, 0][None], buf[0, 1][None], rate)
        high = halo_flux(kk[n - 1:], tt[n - 1:], buf[1, 0][None], buf[1, 1][None], rate)
        return jnp.concatenate([flux[:1] + low, flux[1:n - 1], flux[n - 1:] + high], axis=0)

    flux_v[...] = with_halo(flux_z, k_zy, t_zy, hzr, VERTICAL_RATE).reshape(lines, cx)
    flux_y = with_halo(flux_y, k_yz, t_yz, hyr, LATERAL_RATE) + yz(flux_v)
    residual = flux_x + flux_y.reshape(lines, cx).T

    r_x = apply_stages(stages_x, inv_x, residual)
    put3(xb, me["gx"], (r_x[:1] + 2.0 * t_x[:1], r_x[cx - 1:] + 2.0 * t_x[cx - 1:]))
    gxb.start()

    if line_z:
        pl.semaphore_wait(relay_z, count_z)
    gzm.start()
    glab.start()
    gxm.wait()
    elim_x = chain_factor([tuple(get(xm, i, j) for j in range(3)) for i in range(nx)])
    gxb.wait()

    def join(buf, n, elim, r, first, last, here):
        if buf is zb:
            firsts, lasts = [zb[i, :cy][None] for i in range(n)], [zb[i, 24:40][None] for i in range(n)]
        else:
            firsts, lasts = [get(buf, i, 0) for i in range(n)], [get(buf, i, 1) for i in range(n)]
        qs = chain_flux(elim, firsts, lasts)
        return r + pick(qs, here - 1) * first - pick(qs, here) * last, qs

    step, _ = join(xb, nx, elim_x, r_x, first_x, last_x, me["gx"])
    r_y = apply_stages(stages_y, inv_y, step.T.reshape(cy, cz, cx))
    put3(yb, me["gy"], (r_y[:1], r_y[cy - 1:]))
    gyb.start()

    gym.wait()
    elim_y = chain_factor([tuple(get(ym, i, j) for j in range(3)) for i in range(ny)])
    gyb.wait()
    step, _ = join(yb, ny, elim_y, r_y, first_y, last_y, me["gy"])
    for y in range(cy):
        flux_v[pl.ds(y, cz, stride=cy), :] = step[y]
    rhs_z = flux_v[...].reshape(cz, cy, cx)
    r_z = apply_stages(stages_z, inv_z, rhs_z)
    zb[me["gz"], 0:cy] = r_z[0]
    zb[me["gz"], 24:40] = r_z[cz - 1]
    columns = jnp.sum(t_zy + rhs_z, axis=0)
    for i in range(cy // TY):
        zb[me["gz"], 16 + i:17 + i] = jnp.sum(columns[i * TY:(i + 1) * TY], axis=0, keepdims=True)
    gzb.start()

    gzm.wait()
    elim_z = chain_factor([tuple(zm[i, j * cy:(j + 1) * cy][None] for j in (2, 0, 1)) for i in range(nz)])
    glab.wait()
    width = cbuf.shape[-1] if len(cbuf.shape) == 3 else 128
    ids = lax.broadcasted_iota(jnp.int32, (8, width), 1).astype(jnp.float32)

    def onehot(labels):
        return jnp.concatenate([labels] * (width // 128), axis=1) == ids

    in_tile = lanes8 // TX == rows8 % 4
    gzb.wait()
    step, qs = join(zb, nz, elim_z, r_z, first_z, last_z, me["gz"])

    total = jnp.zeros((8, width), jnp.float32)
    for i in range(nz):
        cells = jnp.zeros((cy, cx), jnp.float32)
        if i > 0:
            cells = cells + qs[i - 1][0]
        if i < nz - 1:
            cells = cells - qs[i][0]
        upper = zb[i, 16:17] + jnp.sum(cells[:TY], axis=0, keepdims=True)
        lower = zb[i, 17:18] + jnp.sum(cells[TY:], axis=0, keepdims=True)
        tiles = jnp.where(in_tile, jnp.where(rows8 < 4, upper, lower), 0.0)
        sums = jnp.sum(tiles, axis=1, keepdims=True)
        total = total + jnp.where(onehot(lab[i]), sums, 0.0)
    total = jnp.sum(total, axis=0, keepdims=True)
    base = 0
    for j, axes in enumerate(stages_c):
        n, here = place(axes)
        part = Gather(cbuf.at[pl.ds(base, n)], axes, sems[14 + 2 * j], sems[15 + 2 * j])
        cbuf[base + here, 0:1] = total
        part.start()
        if j == 0:
            next_ref[...] = (t_zy + step).reshape(lines, cx)
        part.wait()
        total = cbuf[base, 0:1]
        for i in range(1, n):
            total = total + cbuf[base + i, 0:1]
        base += n

    mean = total / (4 * cz * TY * TX)
    leak = dens_ref[...] * jnp.exp(LEAK_SLOPE * mean[:, :clusters])
    power = jnp.sum(jnp.where(onehot(own_label)[:, :clusters], leak, 0.0), axis=1, keepdims=True)
    spread = jnp.where(in_tile, power, 0.0)
    upper = jnp.sum(spread[:4], axis=0, keepdims=True)
    lower = jnp.sum(spread[4:], axis=0, keepdims=True)
    rows16 = lax.broadcasted_iota(jnp.int32, (cy, cx), 0)
    layer = jnp.where(rows16 < TY, upper, lower)
    force_ref[...] = (f_v[...].reshape(cz, cy, cx) + layer[None]).reshape(lines, cx)

    for has, c, r in halos:
        pl.when(has)(c.wait_send)
    for has, c in finish:
        Gather.do(has, c.wait_send)


def per_device(sizes, thermal_field, forcing_per_step, substance_label, thermal_conductivities,
               patch_group_label, drain_power_density):
    nx, ny, nz = sizes
    shape = thermal_field.shape
    cz, cy, cx = shape
    lines = cz * cy
    clusters = drain_power_density.shape[0]
    width = -(-clusters // 128) * 128
    f32 = jnp.float32
    flat = lambda v: v.reshape(lines, cx)
    vm = lambda *s: pltpu.VMEM(s, f32)
    dma = pltpu.SemaphoreType.DMA
    small = nx * ny <= 16
    csizes = [nx * ny] if small else [nx, ny]
    sems = []
    for n in [nx, ny, nz, nx, ny, nz, nz] + csizes:
        sems += [dma((max(n - 1, 1),)), dma((n,))]
    any_spec = pl.BlockSpec(memory_space=pl.ANY)
    new, force = pl.pallas_call(
        functools.partial(kernel, sizes, clusters),
        out_shape=[pltpu.VMEM((lines, cx), f32)] * 2,
        in_specs=[any_spec] * 6,
        out_specs=[pl.BlockSpec(memory_space=pltpu.VMEM)] * 2,
        scratch_shapes=[
            pltpu.SMEM(thermal_conductivities.shape, f32), pltpu.SMEM(patch_group_label.shape, jnp.int32),
            vm(1, clusters),
            vm(lines, cx), vm(lines, cx), pltpu.VMEM((lines, cx), jnp.int32), vm(lines, cx), vm(lines, cx),
            vm(2, 2, cz, cx), vm(2, 2, cz, cx), vm(2, 2, cy, cx), vm(2, 2, cy, cx),
            vm(nx, 8, lines), vm(ny, 3, cz, cx), vm(nz, 48, cx),
            vm(nx, 8, lines), vm(ny, 2, cz, cx), vm(nz, 40, cx),
            vm(nz, 8, 128), vm(sum(csizes), 1, width),
            dma((6,)), dma((4,)), dma((4,)), pltpu.SemaphoreType.REGULAR, pltpu.SemaphoreType.REGULAR,
        ] + sems,
        compiler_params=pltpu.CompilerParams(collective_id=0, has_side_effects=True),
    )(thermal_conductivities, patch_group_label, drain_power_density.reshape(1, clusters),
      flat(thermal_field), flat(forcing_per_step), flat(substance_label))
    return new.reshape(shape), force.reshape(shape)


def solution(mesh):
    block = P("gz", "gy", "gx")
    return jax.shard_map(
        functools.partial(per_device, tuple(mesh.shape[axis] for axis in AXES)),
        mesh=mesh, in_specs=(block, block, block, P(), block, P()), out_specs=(block, block), check_vma=False,
    )
```
